512 devices in a mesh: lon: 32 (over x, z_hi, core), lat: 16 (over y, z_lo).
Axes of the slice: x: 4, y: 8, z: 8 (z_hi: 4, z_lo: 2; z = z_hi * 2 + z_lo), core: 2. Of those that a mesh axis runs over, the one named last changes fastest.
Arguments:
- queries: bfloat16 [128, 512, 1536], P('lat', 'lon'), may hold values from -24 to 24
- keys: bfloat16 [128, 512, 1536], P('lat', 'lon'), may hold values from -24 to 24
- values: bfloat16 [128, 512, 1536], P('lat', 'lon'), may hold values from -6 to 6
- out_grad: bfloat16 [128, 512, 1536], P('lat', 'lon'), may hold values from -6 to 6
- neighbours: int32 [512, 5], replicated, may hold values from -1 to 511, as said below
- partner: int32 [2, 32], replicated, may hold values from 0 to 31, as said below
Outputs:
- attended: bfloat16 [128, 512, 1536], P('lat', 'lon')
- grad_queries: bfloat16 [128, 512, 1536], P('lat', 'lon')
- grad_keys: bfloat16 [128, 512, 1536], P('lat', 'lon')
- grad_values: bfloat16 [128, 512, 1536], P('lat', 'lon')
The draws below stay inside these ranges and needn't reach their ends.
Inputs may be any that keep to these rules, and one draw needn't show every extreme that they name: `neighbours`: row t = b * 32 + s lists, in some order and padded with -1, distinct tiles: t itself always, and any of b * 32 + (s - 1) mod 32, b * 32 + (s + 1) mod 32, t - 32 where b > 0 and t + 32 where b < 15. Rows of the first and the last band list all of those that exist. Each row is a permutation of the strips, and partner[j, s] - s - 16 is -1, 0 or 1 modulo 32.
All inputs are finite; a program needn't handle non-finite values.
Results may differ from the reference program's by a relative error of at most 0.022.
Values may be sent and summed in bfloat16 or wider, within the bound.
A program may use at most 64 MiB of HBM per device.

```python
import jax
import jax.numpy as jnp
from jax import lax

H = 12
DH = 128
TR = 8
TC = 16
HD = 1536
STRIPS = 32
BANDS = 16
TILES = 512
ROWS = 128
COLS = 512


def query_key_pair(key):
    base = jax.random.fold_in(key, 31)
    first, second = jax.random.split(base, 2)
    shape = (ROWS, COLS, H, DH)
    query_vals = jnp.clip(jax.random.normal(first, shape, jnp.float32), -4.0, 4.0)
    key_vals = jnp.clip(jax.random.normal(second, shape, jnp.float32), -4.0, 4.0)
    query_vals = query_vals.reshape(ROWS, COLS, H * DH).astype(jnp.bfloat16)
    key_vals = key_vals.reshape(ROWS, COLS, H * DH).astype(jnp.bfloat16)
    return (query_vals, key_vals)


def draw_queries(key, part):
    return query_key_pair(key)[0]


def draw_keys(key, part):
    return query_key_pair(key)[1]


def draw_neighbours(key, part):
    base = jax.random.fold_in(key, 47)
    keep_key, order_key = jax.random.split(base, 2)
    band_ids = jnp.arange(BANDS)[:, None]
    strip_ids = jnp.arange(STRIPS)[None, :]
    own_ids = band_ids * STRIPS + strip_ids
    west_ids = band_ids * STRIPS + (strip_ids - 1) % STRIPS
    east_ids = band_ids * STRIPS + (strip_ids + 1) % STRIPS
    north_ids = jnp.where(band_ids > 0, own_ids - STRIPS, -1)
    south_ids = jnp.where(band_ids < BANDS - 1, own_ids + STRIPS, -1)
    polar_band = (band_ids == 0) | (band_ids == BANDS - 1)
    keeping = jax.random.randint(keep_key, (BANDS, STRIPS, 4), 0, 2)
    keeping = jnp.where(polar_band[:, :, None], 1, keeping)
    others = jnp.stack([west_ids, east_ids, north_ids, south_ids], axis=-1)
    others = jnp.where(keeping == 1, others, -1)
    table = jnp.concatenate([own_ids[:, :, None], others], axis=-1).reshape(TILES, 5)
    ranking = jax.random.randint(order_key, (TILES, 5), 0, 1 << 20) * 8 + jnp.arange(5)[None, :]
    ordering = jnp.argsort(ranking, axis=1)
    return jnp.take_along_axis(table, ordering, axis=1).astype(jnp.int32)


def draw_partner(key, part):
    base = jax.random.fold_in(key, 59)
    phase_key, flip_key = jax.random.split(base, 2)
    phase = jax.random.randint(phase_key, (), 0, 2)
    flipping = jax.random.randint(flip_key, (2, STRIPS // 2), 0, 2)
    strip_ids = jnp.arange(STRIPS)
    shifted = (strip_ids - phase) % STRIPS
    pair_ids = shifted // 2
    leading = shifted % 2 == 0
    flip_on = flipping[:, pair_ids]
    offsets = jnp.where(flip_on == 1, jnp.where(leading, 1, -1), 0)
    return ((strip_ids[None, :] + offsets + STRIPS // 2) % STRIPS).astype(jnp.int32)


def level_of(stream_key, extent, cuts, smallest, largest):
    factor_of = 1.0
    for dim, parts in cuts:
        draws = jax.random.uniform(jax.random.fold_in(jax.random.fold_in(stream_key, 6), dim), (parts,), jnp.float32, smallest / len(cuts), largest / len(cuts))
        factor_of = factor_of * jnp.repeat(jnp.exp(draws), extent[dim] // parts).reshape((-1,) + (1,) * (len(extent) - 1 - dim))
    return factor_of


def scatter_about(rng, shape, spread, limit, pieces=(), kind=jnp.bfloat16):
    level = level_of(rng, shape, pieces, -0.22, 0.18) if pieces else 1.0
    result = jax.random.normal(rng, shape, jnp.float32) * spread * level
    return jnp.minimum(jnp.maximum(result, -limit), limit).astype(kind)


def setup_inputs(seed: int = 0) -> dict:
    splits = jax.random.split(jax.random.key(seed), 7)
    queries = draw_queries(jax.random.fold_in(splits[6], 71), 0)
    keys = draw_keys(jax.random.fold_in(splits[6], 71), 0)
    values = scatter_about(splits[2], (ROWS, COLS, HD), 1.0, 6.0, ((0, 16), (1, 32)))
    out_grad = scatter_about(splits[3], (ROWS, COLS, HD), 1.0, 6.0, ((0, 16), (1, 32)))
    neighbours = draw_neighbours(jax.random.fold_in(splits[6], 71), 0)
    partner = draw_partner(jax.random.fold_in(splits[6], 71), 0)
    return {"queries": queries, "keys": keys, "values": values, "out_grad": out_grad, "neighbours": neighbours, "partner": partner}


def to_tiles(array):
    shaped = array.reshape(BANDS, TR, STRIPS, TC, H, DH).transpose(0, 2, 1, 3, 4, 5)
    return shaped.reshape(BANDS * STRIPS, TR * TC, H, DH)


def from_tiles(array):
    shaped = array.reshape(BANDS, STRIPS, TR, TC, H * DH).transpose(0, 2, 1, 3, 4)
    return shaped.reshape(TR * BANDS, TC * STRIPS, H * DH)


def reference(queries, keys, values, out_grad, neighbours, partner):
    scale = DH ** -0.5
    tile_query = to_tiles(queries)
    tile_key = to_tiles(keys)
    tile_value = to_tiles(values)
    tile_grad = to_tiles(out_grad)

    def per_tile(carry, index):
        key_total, value_total = carry
        band_id = index // STRIPS
        strip_id = index % STRIPS
        partner_row = jnp.where(band_id == 0, partner[0], partner[1])
        polar_band = (band_id == 0) | (band_id == BANDS - 1)
        extra = jnp.where(polar_band, band_id * STRIPS + partner_row[strip_id], -1).astype(jnp.int32)
        links = jnp.concatenate([neighbours[index].astype(jnp.int32), extra[None]])
        valid = links >= 0
        safe = jnp.where(valid, links, 0).astype(jnp.int32)
        near_keys = tile_key[safe].astype(jnp.float32)
        near_values = tile_value[safe].astype(jnp.float32)
        query = tile_query[index].astype(jnp.float32)
        cotan = tile_grad[index].astype(jnp.float32)
        scores = jnp.einsum('qhd,jkhd->hqjk', query, near_keys) * scale
        scores = jnp.where(valid[None, None, :, None], scores, -jnp.inf)
        highest = jnp.max(scores, axis=(2, 3), keepdims=True)
        total = jnp.sum(jnp.exp(scores - highest), axis=(2, 3), keepdims=True)
        log_norm = highest + jnp.log(total)
        probability = jnp.exp(scores - log_norm)
        weights = probability.astype(jnp.bfloat16).astype(jnp.float32)
        attended = jnp.einsum('hqjk,jkhd->qhd', weights, near_values).astype(jnp.bfloat16)
        delta = jnp.sum(cotan * attended.astype(jnp.float32), axis=-1)
        dprob = jnp.einsum('qhd,jkhd->hqjk', cotan, near_values)
        dscore = (probability * (dprob - delta.T[:, :, None, None])).astype(jnp.bfloat16).astype(jnp.float32)
        grad_query = (scale * jnp.einsum('hqjk,jkhd->qhd', dscore, near_keys)).astype(jnp.bfloat16)
        key_part = jnp.einsum('hqjk,qhd->jkhd', dscore, query)
        value_part = jnp.einsum('hqjk,qhd->jkhd', weights, cotan)
        key_total = key_total.at[safe].add(key_part)
        value_total = value_total.at[safe].add(value_part)
        return (key_total, value_total), (attended, grad_query)

    empty = jnp.zeros((BANDS * STRIPS, TR * TC, H, DH), jnp.float32)
    (key_total, value_total), (attended, grad_query) = lax.scan(
        per_tile, (empty, empty), jnp.arange(BANDS * STRIPS, dtype=jnp.int32))
    grad_keys = (scale * key_total).astype(jnp.bfloat16)
    grad_values = value_total.astype(jnp.bfloat16)
    return from_tiles(attended), from_tiles(grad_query), from_tiles(grad_keys), from_tiles(grad_values)
```

```python
import functools

import jax
import jax.numpy as jnp
from jax import lax
from jax.experimental import pallas as pl
from jax.experimental.pallas import tpu as pltpu
from jax.sharding import PartitionSpec as P

DH = 128
NEG = -1e30
AHEAD = 4
LAG = 3
MESH = pl.DeviceIdType.MESH

OWN, WEST, EAST, MATE, FAR = range(5)


def nt(a, b):
    return lax.dot_general(a, b, (((1,), (1,)), ((), ())), preferred_element_type=jnp.float32)


def nn(a, b):
    return lax.dot_general(a, b, (((1,), (0,)), ((), ())), preferred_element_type=jnp.float32)


def kernel(
    heads, lon, lat,
    q_hbm, k_hbm, v_hbm, g_hbm, nb_hbm, pt_hbm,
    o_hbm, dq_hbm, dk_hbm, dv_hbm,
    buf, st, far_st, pick, hop, out, nb, pt, bias, flag,
    ld_sem, tb_sem, rx_sem, tx_sem, strx_sem, sttx_sem, picktx_sem, hoprx_sem, hoptx_sem, out_sem,
):
    s = lax.axis_index("lon")
    b = lax.axis_index("lat")
    core = s % 2
    odd = b % 2
    mate_b = b + 1 - 2 * odd
    far_b = b - 1 + 2 * odd
    relay_b = b + 2 - 4 * odd
    on_s = s + 1 - 2 * core
    off_s = (s + 2 * core - 1 + lon) % lon
    west_s = (s + lon - 1) % lon
    east_s = (s + 1) % lon
    quarter = lon // 4
    opp = (s + lon // 2) % lon
    opp_w = (opp + lon - 1) % lon
    opp_e = (opp + 1) % lon
    on_slot = 1 + core
    off_slot = 2 - core
    heavy = odd == core
    has_relay = (relay_b >= 0) & (relay_b < lat)
    has_far = (far_b >= 0) & (far_b < lat)
    polar = (b == 0) | (b == lat - 1)
    scale = DH ** -0.5

    def dev(band, strip):
        return {"lat": band, "lon": strip}

    peers = [
        (None, dev(mate_b, s)),
        (None, dev(b, on_s)),
        (None, dev(b, off_s)),
        (has_far, dev(far_b, s)),
        (b + 2 < lat, dev(b + 2, s)),
        (b >= 2, dev(b - 2, s)),
        (heavy, dev(mate_b, off_s)),
        (polar, dev(b, (s + quarter) % lon)),
        (polar, dev(b, (s + lon - quarter) % lon)),
        (polar, dev(b, opp_w)),
        (polar, dev(b, opp)),
        (polar, dev(b, opp_e)),
    ]

    def columns(h):
        return pl.ds(pl.multiple_of(h * DH, DH), DH)

    sources = ((k_hbm, v_hbm), (q_hbm, g_hbm))

    def load(kind, which, h):
        return pltpu.make_async_copy(
            sources[kind][which].at[:, columns(h)], buf.at[kind, OWN, h, which], ld_sem.at[kind, which, h]
        )

    @pl.loop(0, heads)
    def _(h):
        for kind in range(2):
            for which in range(2):
                load(kind, which, h).start()

    tables = (pltpu.make_async_copy(nb_hbm, nb, tb_sem.at[0]), pltpu.make_async_copy(pt_hbm, pt, tb_sem.at[1]))
    for copy in tables:
        copy.start()

    barrier = pltpu.get_barrier_semaphore()
    expected = 0
    for cond, device in peers:
        if cond is None:
            pl.semaphore_signal(barrier, inc=1, device_id=device, device_id_type=MESH)
            expected = expected + 1
        else:
            @pl.when(cond)
            def _():
                pl.semaphore_signal(barrier, inc=1, device_id=device, device_id_type=MESH)
            expected = expected + jnp.where(cond, 1, 0)
    pl.semaphore_wait(barrier, expected)

    def send(src, dst, tx, rx, device):
        return pltpu.make_async_remote_copy(
            src_ref=src, dst_ref=dst, send_sem=tx, recv_sem=rx, device_id=device, device_id_type=MESH
        )

    def chunk(kind, from_slot, to_slot, h, route, device):
        return send(
            buf.at[kind, from_slot, h], buf.at[kind, to_slot, h],
            tx_sem.at[kind, route, h], rx_sem.at[kind, to_slot, h], device,
        )

    def to_mate(kind, h):
        return chunk(kind, OWN, MATE, h, 0, dev(mate_b, s))

    def to_core(kind, h):
        return chunk(kind, OWN, on_slot, h, 1, dev(b, on_s))

    def to_side(kind, h):
        return chunk(kind, OWN, off_slot, h, 2, dev(b, off_s))

    def mate_to_band(kind, h):
        return chunk(kind, MATE, FAR, h, 3, dev(relay_b, s))

    def mate_to_side(kind, h):
        return chunk(kind, MATE, off_slot, h, 4, dev(mate_b, off_s))

    def arrival(kind, slot, h):
        return chunk(kind, slot, slot, h, 0, dev(mate_b, s))

    def around(kind, strip, steps):
        return (strip + (steps * quarter if kind == 0 else lon - steps * quarter)) % lon

    def pick_to_hop(kind, h):
        return send(
            pick.at[kind, h], hop.at[kind, h], picktx_sem.at[kind, h], hoprx_sem.at[kind, h], dev(b, around(kind, s, 1))
        )

    def hop_to_far(kind, h):
        return send(
            hop.at[kind, h], buf.at[kind, FAR, h], hoptx_sem.at[kind, h], rx_sem.at[kind, FAR, h],
            dev(b, around(kind, s, 1)),
        )

    def stat(to_slot, h, route, device):
        return send(st.at[OWN, h], st.at[to_slot, h], sttx_sem.at[route, h], strx_sem.at[to_slot, h], device)

    def stat_sends(h):
        return (
            (None, stat(EAST, h, 0, dev(b, west_s))),
            (None, stat(WEST, h, 1, dev(b, east_s))),
            (None, stat(MATE, h, 2, dev(mate_b, s))),
            (has_far, stat(FAR, h, 3, dev(far_b, s))),
            (polar, stat(FAR, h, 3, dev(b, opp))),
            (polar, stat(6, h, 4, dev(b, opp_w))),
            (polar, stat(5, h, 5, dev(b, opp_e))),
        )

    def guarded(cond, action):
        if cond is None:
            action()
        else:
            pl.when(cond)(action)

    def within(h):
        return (h >= 0) & (h < heads)

    def send_own(kind, h):
        if kind == 0:
            for k in range(2):
                for which in range(2):
                    load(k, which, h).wait()
        to_mate(kind, h).start()
        to_core(kind, h).start()
        pl.when(heavy)(lambda: to_side(kind, h).start())

    def own_sends(t):
        for kind, h in ((0, t + AHEAD), (1, t + AHEAD - LAG)):
            pl.when(within(h))(functools.partial(send_own, kind, h))

    def relay(kind, h):
        arrival(kind, MATE, h).wait_recv()
        pl.when(heavy)(lambda: mate_to_side(kind, h).start())
        pl.when(has_relay)(lambda: mate_to_band(kind, h).start())

    def collect(kind, h):
        arrival(kind, WEST, h).wait_recv()
        arrival(kind, EAST, h).wait_recv()

        @pl.when(polar)
        def _():
            for which in range(2):
                total = buf[kind, OWN, h, which].astype(jnp.float32) * flag[3 * kind, 0:1, :]
                total += buf[kind, WEST, h, which].astype(jnp.float32) * flag[3 * kind + 1, 0:1, :]
                total += buf[kind, EAST, h, which].astype(jnp.float32) * flag[3 * kind + 2, 0:1, :]
                pick[kind, h, which] = total.astype(jnp.bfloat16)
            pick_to_hop(kind, h).start()

    def forward_hop(kind, h):
        pick_to_hop(kind, h).wait_recv()
        hop_to_far(kind, h).start()

    def result(i, h):
        return pltpu.make_async_copy(
            out.at[i, h], (o_hbm, dq_hbm, dk_hbm, dv_hbm)[i].at[:, columns(h)], out_sem.at[i, h]
        )

    def attend(h):
        arrival(0, FAR, h).wait_recv()
        query = buf[1, OWN, h, 0]
        cotan = buf[1, OWN, h, 1]
        keys = buf[0, :, h, 0].reshape(5 * DH, DH)
        values = buf[0, :, h, 1].reshape(5 * DH, DH)
        scores = nt(query, keys) * scale + bias[0, 0:1, :]
        highest = jnp.max(scores, axis=1, keepdims=True)
        grown = jnp.exp(scores - highest)
        total = jnp.sum(grown, axis=1, keepdims=True)
        probability = grown * (1.0 / total)
        attended = nn(probability.astype(jnp.bfloat16), values).astype(jnp.bfloat16)
        delta = jnp.sum(cotan.astype(jnp.float32) * attended.astype(jnp.float32), axis=1, keepdims=True)
        lse = highest + jnp.log(total)
        lane = lax.broadcasted_iota(jnp.int32, (DH, DH), 1)
        both = jnp.where(lane < 4, jnp.broadcast_to(lse, (DH, DH)), jnp.broadcast_to(delta, (DH, DH)))
        st[OWN, h] = jnp.transpose(both)[0:8, :]
        for cond, copy in stat_sends(h):
            guarded(cond, copy.start)
        out[0, h] = attended
        result(0, h).start()
        dprob = nt(cotan, values)
        dscore = (probability * (dprob - delta)).astype(jnp.bfloat16)
        out[1, h] = (nn(dscore, keys) * scale).astype(jnp.bfloat16)
        result(1, h).start()

    def spread(h):
        arrival(1, FAR, h).wait_recv()
        for slot in (WEST, EAST, MATE, FAR):
            stat(slot, h, 0, dev(mate_b, s)).wait_recv()
        pl.when(~polar)(lambda: far_st.__setitem__(Ellipsis, st[FAR, h]))

        @pl.when(polar)
        def _():
            for slot in (5, 6):
                stat(slot, h, 0, dev(mate_b, s)).wait_recv()
            chosen = jnp.where(flag[6, :, :] > 0.5, st[5, h], st[FAR, h])
            far_st[...] = jnp.where(flag[7, :, :] > 0.5, st[6, h], chosen)

        rows = [st[slot, h] for slot in (OWN, WEST, EAST, MATE)] + [far_st[...]]
        shift = bias[1, 0:1, :] - jnp.concatenate([r[0:1, :] for r in rows], axis=1)
        delta = jnp.concatenate([r[4:5, :] for r in rows], axis=1)
        key = buf[0, OWN, h, 0]
        value = buf[0, OWN, h, 1]
        queries = buf[1, :, h, 0].reshape(5 * DH, DH)
        cotans = buf[1, :, h, 1].reshape(5 * DH, DH)
        probability = jnp.exp(nt(key, queries) * scale + shift)
        dscore = (probability * (nt(value, cotans) - delta)).astype(jnp.bfloat16)
        out[3, h] = nn(probability.astype(jnp.bfloat16), cotans).astype(jnp.bfloat16)
        result(3, h).start()
        out[2, h] = (nn(dscore, queries) * scale).astype(jnp.bfloat16)
        result(2, h).start()

    @pl.loop(0, AHEAD)
    def _(t):
        own_sends(t - AHEAD)

    for copy in tables:
        copy.wait()

    ids = [b * lon + s, b * lon + west_s, b * lon + east_s, mate_b * lon + s, far_b * lon + s]
    table = nb[...].astype(jnp.float32)
    lanes = lax.broadcasted_iota(jnp.int32, table.shape, 1)

    def lists(tile, other):
        row = jnp.sum(jnp.where(lanes == tile, table, 0.0), axis=1, keepdims=True)
        hit = jnp.where(row == other.astype(jnp.float32), 1.0, 0.0)
        return jnp.max(hit, axis=0, keepdims=True)

    def as_bias(parts):
        polar_one = jnp.where(polar, 1.0, 0.0)
        parts[FAR] = jnp.maximum(parts[FAR], polar_one)
        whole = jnp.concatenate([jnp.broadcast_to(p, (8, DH)) for p in parts], axis=1)
        return jnp.where(whole > 0.5, 0.0, NEG)

    bias[0] = as_bias([lists(ids[0], other) for other in ids])
    bias[1] = as_bias([lists(other, ids[0]) for other in ids])

    @pl.when(polar)
    def _():
        across = pt[...].astype(jnp.float32)
        strip_of = lax.broadcasted_iota(jnp.int32, across.shape, 1)
        row_of = lax.broadcasted_iota(jnp.int32, across.shape, 0)
        mine = jnp.where(b == 0, 0, 1)

        def partner_is(strip, other):
            here = jnp.where((row_of == mine) & (strip_of == strip), across, 0.0)
            value = jnp.sum(jnp.sum(here, axis=1, keepdims=True), axis=0, keepdims=True)
            return jnp.broadcast_to(jnp.where(value == other.astype(jnp.float32), 1.0, 0.0), (8, DH))

        pairs = ((partner_is(opp, west_s), partner_is(opp, east_s)), (partner_is(west_s, opp), partner_is(east_s, opp)))
        for kind, (west, east) in enumerate(pairs):
            flag[3 * kind] = 1.0 - west - east
            flag[3 * kind + 1] = west
            flag[3 * kind + 2] = east
        flag[6] = partner_is(opp_w, s)
        flag[7] = partner_is(opp_e, s)

    late = jnp.where(polar, 2, 0)

    @pl.loop(0, heads + LAG + 2)
    def _(t):
        own_sends(t)
        now = ((0, t), (1, t - LAG))
        for kind, h in now:
            pl.when(within(h))(functools.partial(relay, kind, h))
        for kind, h in now:
            pl.when(within(h))(functools.partial(collect, kind, h))
        for kind, h in now:
            pl.when(polar & within(h - 1))(functools.partial(forward_hop, kind, h - 1))
        pl.when(within(t - late))(lambda: attend(t - late))
        pl.when(within(t - late - LAG))(lambda: spread(t - late - LAG))

    @pl.loop(0, heads)
    def _(h):
        for kind in range(2):
            to_mate(kind, h).wait_send()
            to_core(kind, h).wait_send()

            @pl.when(heavy)
            def _():
                to_side(kind, h).wait_send()
                mate_to_side(kind, h).wait_send()

            pl.when(has_relay)(lambda: mate_to_band(kind, h).wait_send())

            @pl.when(polar)
            def _():
                pick_to_hop(kind, h).wait_send()
                hop_to_far(kind, h).wait_send()

        for cond, copy in stat_sends(h):
            guarded(cond, copy.wait_send)
        for i in range(4):
            result(i, h).wait()


def body(queries, keys, values, out_grad, neighbours, partner):
    lon = lax.axis_size("lon")
    lat = lax.axis_size("lat")
    shape = queries.shape
    tokens = shape[0] * shape[1]
    width = shape[2]
    heads = width // DH
    flat = [a.reshape(tokens, width) for a in (queries, keys, values, out_grad)]
    anywhere = pl.BlockSpec(memory_space=pl.ANY)
    bf16 = jnp.bfloat16
    f32 = jnp.float32
    dma = pltpu.SemaphoreType.DMA
    tile = (DH, DH)
    results = pl.pallas_call(
        functools.partial(kernel, heads, lon, lat),
        out_shape=[jax.ShapeDtypeStruct((tokens, width), bf16)] * 4,
        in_specs=[anywhere] * 6,
        out_specs=[anywhere] * 4,
        scratch_shapes=[
            pltpu.VMEM((2, 5, heads, 2) + tile, bf16),
            pltpu.VMEM((7, heads, 8, DH), f32),
            pltpu.VMEM((8, DH), f32),
            pltpu.VMEM((2, heads, 2) + tile, bf16),
            pltpu.VMEM((2, heads, 2) + tile, bf16),
            pltpu.VMEM((4, heads) + tile, bf16),
            pltpu.VMEM(neighbours.shape[::-1], jnp.int32),
            pltpu.VMEM(partner.shape, jnp.int32),
            pltpu.VMEM((2, 8, 5 * DH), f32),
            pltpu.VMEM((8, 8, DH), f32),
            dma((2, 2, heads)),
            dma((2,)),
            dma((2, 5, heads)),
            dma((2, 5, heads)),
            dma((7, heads)),
            dma((6, heads)),
            dma((2, heads)),
            dma((2, heads)),
            dma((2, heads)),
            dma((4, heads)),
        ],
        compiler_params=pltpu.CompilerParams(
            collective_id=0, has_side_effects=True, vmem_limit_bytes=48 * 1024 * 1024
        ),
        name="tile_attention",
    )(*flat, neighbours.T, partner)
    return tuple(r.reshape(shape) for r in results)


def solution(mesh):
    tiled = P("lat", "lon", None)
    return jax.shard_map(
        body,
        mesh=mesh,
        in_specs=(tiled, tiled, tiled, tiled, P(), P()),
        out_specs=(tiled, tiled, tiled, tiled),
        check_vma=False,
    )
```

```python
import functools

import jax
import jax.numpy as jnp
from jax import lax
from jax.experimental import pallas as pl
from jax.experimental.pallas import tpu as pltpu
from jax.sharding import PartitionSpec as P

DH = 128
NEG = -1e30
AHEAD = 5
SIDE = 2
LAG = 3
LATE = 2
MESH = pl.DeviceIdType.MESH

OWN, WEST, EAST, MATE, FAR = range(5)


def nt(a, b):
    return lax.dot_general(a, b, (((1,), (1,)), ((), ())), preferred_element_type=jnp.float32)


def nn(a, b):
    return lax.dot_general(a, b, (((1,), (0,)), ((), ())), preferred_element_type=jnp.float32)


def kernel(
    heads, lon, lat,
    q_hbm, k_hbm, v_hbm, g_hbm, nb_hbm, pt_hbm,
    o_hbm, dq_hbm, dk_hbm, dv_hbm,
    buf, st, far_st, pick, out, nb, pt, bias, flag,
    ld_sem, tb_sem, rx_sem, tx_sem, strx_sem, sttx_sem, picktx_sem, out_sem,
):
    s = lax.axis_index("lon")
    b = lax.axis_index("lat")
    core = s % 2
    odd = b % 2
    mate_b = b + 1 - 2 * odd
    far_b = b - 1 + 2 * odd
    relay_b = b + 2 - 4 * odd
    on_s = s + 1 - 2 * core
    off_s = (s + 2 * core - 1 + lon) % lon
    west_s = (s + lon - 1) % lon
    east_s = (s + 1) % lon
    opp = (s + lon // 2) % lon
    opp_w = (opp + lon - 1) % lon
    opp_e = (opp + 1) % lon
    on_slot = 1 + core
    off_slot = 2 - core
    heavy = odd == core
    has_relay = (relay_b >= 0) & (relay_b < lat)
    has_far = (far_b >= 0) & (far_b < lat)
    polar = (b == 0) | (b == lat - 1)
    scale = DH ** -0.5

    def dev(band, strip):
        return {"lat": band, "lon": strip}

    peers = [
        (None, dev(mate_b, s)),
        (None, dev(b, on_s)),
        (None, dev(b, off_s)),
        (has_far, dev(far_b, s)),
        (b + 2 < lat, dev(b + 2, s)),
        (b >= 2, dev(b - 2, s)),
        (heavy, dev(mate_b, off_s)),
        (polar, dev(b, opp_w)),
        (polar, dev(b, opp)),
        (polar, dev(b, opp_e)),
    ]

    def columns(h):
        return pl.ds(pl.multiple_of(h * DH, DH), DH)

    sources = ((k_hbm, v_hbm), (q_hbm, g_hbm))

    def load(kind, which, h):
        return pltpu.make_async_copy(
            sources[kind][which].at[:, columns(h)], buf.at[kind, OWN, h, which], ld_sem.at[kind, which, h]
        )

    @pl.loop(0, heads)
    def _(h):
        for kind in range(2):
            for which in range(2):
                load(kind, which, h).start()

    tables = (pltpu.make_async_copy(nb_hbm, nb, tb_sem.at[0]), pltpu.make_async_copy(pt_hbm, pt, tb_sem.at[1]))
    for copy in tables:
        copy.start()

    barrier = pltpu.get_barrier_semaphore()
    expected = 0
    for cond, device in peers:
        if cond is None:
            pl.semaphore_signal(barrier, inc=1, device_id=device, device_id_type=MESH)
            expected = expected + 1
        else:
            @pl.when(cond)
            def _():
                pl.semaphore_signal(barrier, inc=1, device_id=device, device_id_type=MESH)
            expected = expected + jnp.where(cond, 1, 0)
    pl.semaphore_wait(barrier, expected)

    def send(src, dst, tx, rx, device):
        return pltpu.make_async_remote_copy(
            src_ref=src, dst_ref=dst, send_sem=tx, recv_sem=rx, device_id=device, device_id_type=MESH
        )

    def chunk(kind, from_slot, to_slot, h, route, device):
        return send(
            buf.at[kind, from_slot, h], buf.at[kind, to_slot, h],
            tx_sem.at[kind, route, h], rx_sem.at[kind, to_slot, h], device,
        )

    def to_mate(kind, h):
        return chunk(kind, OWN, MATE, h, 0, dev(mate_b, s))

    def to_core(kind, h):
        return chunk(kind, OWN, on_slot, h, 1, dev(b, on_s))

    def to_side(kind, h):
        return chunk(kind, OWN, off_slot, h, 2, dev(b, off_s))

    def mate_to_band(kind, h):
        return chunk(kind, MATE, FAR, h, 3, dev(relay_b, s))

    def mate_to_side(kind, h):
        return chunk(kind, MATE, off_slot, h, 4, dev(mate_b, off_s))

    def arrival(kind, slot, h):
        return chunk(kind, slot, slot, h, 0, dev(mate_b, s))

    def pick_to_far(kind, h):
        return send(
            pick.at[kind, h], buf.at[kind, FAR, h], picktx_sem.at[kind, h], rx_sem.at[kind, FAR, h], dev(b, opp)
        )

    def stat(to_slot, h, route, device):
        return send(st.at[OWN, h], st.at[to_slot, h], sttx_sem.at[route, h], strx_sem.at[to_slot, h], device)

    def stat_sends(h):
        return (
            (None, stat(EAST, h, 0, dev(b, west_s))),
            (None, stat(WEST, h, 1, dev(b, east_s))),
            (None, stat(MATE, h, 2, dev(mate_b, s))),
            (has_far, stat(FAR, h, 3, dev(far_b, s))),
            (polar, stat(FAR, h, 3, dev(b, opp))),
            (polar, stat(6, h, 4, dev(b, opp_w))),
            (polar, stat(5, h, 5, dev(b, opp_e))),
        )

    def guarded(cond, action):
        if cond is None:
            action()
        else:
            pl.when(cond)(action)

    def within(h):
        return (h >= 0) & (h < heads)

    def send_own(kind, h):
        if kind == 0:
            for k in range(2):
                for which in range(2):
                    load(k, which, h).wait()
        to_mate(kind, h).start()
        to_core(kind, h).start()

    def own_sends(t):
        for kind, h in ((0, t + AHEAD), (1, t + AHEAD - LAG)):
            pl.when(within(h))(functools.partial(send_own, kind, h))

    def relay(kind, h):
        pl.when(heavy)(lambda: to_side(kind, h).start())
        arrival(kind, MATE, h).wait_recv()
        pl.when(heavy)(lambda: mate_to_side(kind, h).start())
        pl.when(has_relay)(lambda: mate_to_band(kind, h).start())

    def collect(kind, h):
        arrival(kind, WEST, h).wait_recv()
        arrival(kind, EAST, h).wait_recv()

        @pl.when(polar)
        def _():
            for which in range(2):
                total = buf[kind, OWN, h, which].astype(jnp.float32) * flag[3 * kind, 0:1, :]
                total += buf[kind, WEST, h, which].astype(jnp.float32) * flag[3 * kind + 1, 0:1, :]
                total += buf[kind, EAST, h, which].astype(jnp.float32) * flag[3 * kind + 2, 0:1, :]
                pick[kind, h, which] = total.astype(jnp.bfloat16)
            pick_to_far(kind, h).start()

    def result(i, h):
        return pltpu.make_async_copy(
            out.at[i, h], (o_hbm, dq_hbm, dk_hbm, dv_hbm)[i].at[:, columns(h)], out_sem.at[i, h]
        )

    def attend(h):
        arrival(0, FAR, h).wait_recv()
        query = buf[1, OWN, h, 0]
        cotan = buf[1, OWN, h, 1]
        keys = buf[0, :, h, 0].reshape(5 * DH, DH)
        values = buf[0, :, h, 1].reshape(5 * DH, DH)
        scores = nt(query, keys) * scale + bias[0, 0:1, :]
        highest = jnp.max(scores, axis=1, keepdims=True)
        grown = jnp.exp(scores - highest)
        total = jnp.sum(grown, axis=1, keepdims=True)
        probability = grown * (1.0 / total)
        attended = nn(probability.astype(jnp.bfloat16), values).astype(jnp.bfloat16)
        delta = jnp.sum(cotan.astype(jnp.float32) * attended.astype(jnp.float32), axis=1, keepdims=True)
        lse = highest + jnp.log(total)
        lane = lax.broadcasted_iota(jnp.int32, (DH, DH), 1)
        both = jnp.where(lane < 4, jnp.broadcast_to(lse, (DH, DH)), jnp.broadcast_to(delta, (DH, DH)))
        st[OWN, h] = jnp.transpose(both)[0:8, :]
        for cond, copy in stat_sends(h):
            guarded(cond, copy.start)
        out[0, h] = attended
        result(0, h).start()
        dprob = nt(cotan, values)
        dscore = (probability * (dprob - delta)).astype(jnp.bfloat16)
        out[1, h] = (nn(dscore, keys) * scale).astype(jnp.bfloat16)
        result(1, h).start()

    def spread(h):
        arrival(1, FAR, h).wait_recv()
        for slot in (WEST, EAST, MATE, FAR):
            stat(slot, h, 0, dev(mate_b, s)).wait_recv()
        pl.when(~polar)(lambda: far_st.__setitem__(Ellipsis, st[FAR, h]))

        @pl.when(polar)
        def _():
            for slot in (5, 6):
                stat(slot, h, 0, dev(mate_b, s)).wait_recv()
            chosen = jnp.where(flag[6, :, :] > 0.5, st[5, h], st[FAR, h])
            far_st[...] = jnp.where(flag[7, :, :] > 0.5, st[6, h], chosen)

        rows = [st[slot, h] for slot in (OWN, WEST, EAST, MATE)] + [far_st[...]]
        shift = bias[1, 0:1, :] - jnp.concatenate([r[0:1, :] for r in rows], axis=1)
        delta = jnp.concatenate([r[4:5, :] for r in rows], axis=1)
        key = buf[0, OWN, h, 0]
        value = buf[0, OWN, h, 1]
        queries = buf[1, :, h, 0].reshape(5 * DH, DH)
        cotans = buf[1, :, h, 1].reshape(5 * DH, DH)
        probability = jnp.exp(nt(key, queries) * scale + shift)
        dscore = (probability * (nt(value, cotans) - delta)).astype(jnp.bfloat16)
        out[3, h] = nn(probability.astype(jnp.bfloat16), cotans).astype(jnp.bfloat16)
        result(3, h).start()
        out[2, h] = (nn(dscore, queries) * scale).astype(jnp.bfloat16)
        result(2, h).start()

    def relays(t):
        for kind, h in ((0, t + SIDE), (1, t + SIDE - LAG)):
            pl.when(within(h))(functools.partial(relay, kind, h))

    @pl.loop(0, AHEAD)
    def _(t):
        own_sends(t - AHEAD)

    @pl.loop(0, SIDE)
    def _(t):
        relays(t - SIDE)

    for copy in tables:
        copy.wait()

    ids = [b * lon + s, b * lon + west_s, b * lon + east_s, mate_b * lon + s, far_b * lon + s]
    table = nb[...].astype(jnp.float32)
    lanes = lax.broadcasted_iota(jnp.int32, table.shape, 1)

    def lists(tile, other):
        row = jnp.sum(jnp.where(lanes == tile, table, 0.0), axis=1, keepdims=True)
        hit = jnp.where(row == other.astype(jnp.float32), 1.0, 0.0)
        return jnp.max(hit, axis=0, keepdims=True)

    def as_bias(parts):
        polar_one = jnp.where(polar, 1.0, 0.0)
        parts[FAR] = jnp.maximum(parts[FAR], polar_one)
        whole = jnp.concatenate([jnp.broadcast_to(p, (8, DH)) for p in parts], axis=1)
        return jnp.where(whole > 0.5, 0.0, NEG)

    bias[0] = as_bias([lists(ids[0], other) for other in ids])
    bias[1] = as_bias([lists(other, ids[0]) for other in ids])

    @pl.when(polar)
    def _():
        across = pt[...].astype(jnp.float32)
        strip_of = lax.broadcasted_iota(jnp.int32, across.shape, 1)
        row_of = lax.broadcasted_iota(jnp.int32, across.shape, 0)
        mine = jnp.where(b == 0, 0, 1)

        def partner_is(strip, other):
            here = jnp.where((row_of == mine) & (strip_of == strip), across, 0.0)
            value = jnp.sum(jnp.sum(here, axis=1, keepdims=True), axis=0, keepdims=True)
            return jnp.broadcast_to(jnp.where(value == other.astype(jnp.float32), 1.0, 0.0), (8, DH))

        pairs = ((partner_is(opp, west_s), partner_is(opp, east_s)), (partner_is(west_s, opp), partner_is(east_s, opp)))
        for kind, (west, east) in enumerate(pairs):
            flag[3 * kind] = 1.0 - west - east
            flag[3 * kind + 1] = west
            flag[3 * kind + 2] = east
        flag[6] = partner_is(opp_w, s)
        flag[7] = partner_is(opp_e, s)

    late = jnp.where(polar, LATE, 0)

    @pl.loop(0, heads + LAG + LATE)
    def _(t):
        own_sends(t)
        relays(t)
        for kind, h in ((0, t), (1, t - LAG)):
            pl.when(within(h))(functools.partial(collect, kind, h))
        pl.when(within(t - late))(lambda: attend(t - late))
        pl.when(within(t - late - LAG))(lambda: spread(t - late - LAG))

    @pl.loop(0, heads)
    def _(h):
        for kind in range(2):
            to_mate(kind, h).wait_send()
            to_core(kind, h).wait_send()

            @pl.when(heavy)
            def _():
                to_side(kind, h).wait_send()
                mate_to_side(kind, h).wait_send()

            pl.when(has_relay)(lambda: mate_to_band(kind, h).wait_send())

            pl.when(polar)(lambda: pick_to_far(kind, h).wait_send())

        for cond, copy in stat_sends(h):
            guarded(cond, copy.wait_send)
        for i in range(4):
            result(i, h).wait()


def body(queries, keys, values, out_grad, neighbours, partner):
    lon = lax.axis_size("lon")
    lat = lax.axis_size("lat")
    shape = queries.shape
    tokens = shape[0] * shape[1]
    width = shape[2]
    heads = width // DH
    flat = [a.reshape(tokens, width) for a in (queries, keys, values, out_grad)]
    anywhere = pl.BlockSpec(memory_space=pl.ANY)
    bf16 = jnp.bfloat16
    f32 = jnp.float32
    dma = pltpu.SemaphoreType.DMA
    tile = (DH, DH)
    results = pl.pallas_call(
        functools.partial(kernel, heads, lon, lat),
        out_shape=[jax.ShapeDtypeStruct((tokens, width), bf16)] * 4,
        in_specs=[pl.BlockSpec(memory_space=pltpu.HBM)] * 6,
        out_specs=[anywhere] * 4,
        scratch_shapes=[
            pltpu.VMEM((2, 5, heads, 2) + tile, bf16),
            pltpu.VMEM((7, heads, 8, DH), f32),
            pltpu.VMEM((8, DH), f32),
            pltpu.VMEM((2, heads, 2) + tile, bf16),
            pltpu.VMEM((4, heads) + tile, bf16),
            pltpu.VMEM(neighbours.shape[::-1], jnp.int32),
            pltpu.VMEM(partner.shape, jnp.int32),
            pltpu.VMEM((2, 8, 5 * DH), f32),
            pltpu.VMEM((8, 8, DH), f32),
            dma((2, 2, heads)),
            dma((2,)),
            dma((2, 5, heads)),
            dma((2, 5, heads)),
            dma((7, heads)),
            dma((6, heads)),
            dma((2, heads)),
            dma((4, heads)),
        ],
        compiler_params=pltpu.CompilerParams(
            collective_id=0, has_side_effects=True, vmem_limit_bytes=63 * 1024 * 1024
        ),
        name="tile_attention",
    )(*flat, neighbours.T, partner)
    return tuple(r.reshape(shape) for r in results)


def solution(mesh):
    tiled = P("lat", "lon", None)
    return jax.shard_map(
        body,
        mesh=mesh,
        in_specs=(tiled, tiled, tiled, tiled, P(), P()),
        out_specs=(tiled, tiled, tiled, tiled),
        check_vma=False,
    )
```

```python
import functools

import jax
import jax.numpy as jnp
from jax import lax
from jax.experimental import pallas as pl
from jax.experimental.pallas import tpu as pltpu
from jax.sharding import PartitionSpec as P

DH = 128
NEG = -1e30
AHEAD = 5
SIDE = 2
LAG = 8
LATE = 4
FAR_LATE = 6
MESH = pl.DeviceIdType.MESH

OWN, WEST, EAST, MATE, FAR = range(5)


def nt(a, b):
    return lax.dot_general(a, b, (((1,), (1,)), ((), ())), preferred_element_type=jnp.float32)


def nn(a, b):
    return lax.dot_general(a, b, (((1,), (0,)), ((), ())), preferred_element_type=jnp.float32)


def kernel(
    heads, lon, lat,
    q_hbm, k_hbm, v_hbm, g_hbm, nb_hbm, pt_hbm,
    out_o, out_dq, out_dk, out_dv,
    buf, st, far_st, near, pick, nb, pt, bias, flag,
    ld_sem, tb_sem, rx_sem, tx_sem, strx_sem, sttx_sem, picktx_sem,
):
    s = lax.axis_index("lon")
    b = lax.axis_index("lat")
    core = s % 2
    odd = b % 2
    mate_b = b + 1 - 2 * odd
    far_b = b - 1 + 2 * odd
    relay_b = b + 2 - 4 * odd
    on_s = s + 1 - 2 * core
    off_s = (s + 2 * core - 1 + lon) % lon
    west_s = (s + lon - 1) % lon
    east_s = (s + 1) % lon
    opp = (s + lon // 2) % lon
    opp_w = (opp + lon - 1) % lon
    opp_e = (opp + 1) % lon
    on_slot = 1 + core
    off_slot = 2 - core
    heavy = odd == core
    has_relay = (relay_b >= 0) & (relay_b < lat)
    has_far = (far_b >= 0) & (far_b < lat)
    polar = (b == 0) | (b == lat - 1)
    scale = DH ** -0.5

    def dev(band, strip):
        return {"lat": band, "lon": strip}

    peers = [
        (None, dev(mate_b, s)),
        (None, dev(b, on_s)),
        (None, dev(b, off_s)),
        (has_far, dev(far_b, s)),
        (b + 2 < lat, dev(b + 2, s)),
        (b >= 2, dev(b - 2, s)),
        (heavy, dev(mate_b, off_s)),
        (polar, dev(b, opp_w)),
        (polar, dev(b, opp)),
        (polar, dev(b, opp_e)),
    ]

    def columns(h):
        return pl.ds(pl.multiple_of(h * DH, DH), DH)

    sources = ((k_hbm, v_hbm), (q_hbm, g_hbm))

    def load(kind, which, h):
        return pltpu.make_async_copy(
            sources[kind][which].at[:, columns(h)], buf.at[kind, OWN, h, which], ld_sem.at[kind, which, h]
        )

    @pl.loop(0, heads)
    def _(h):
        for kind in range(2):
            for which in range(2):
                load(kind, which, h).start()

    tables = (pltpu.make_async_copy(nb_hbm, nb, tb_sem.at[0]), pltpu.make_async_copy(pt_hbm, pt, tb_sem.at[1]))
    for copy in tables:
        copy.start()

    barrier = pltpu.get_barrier_semaphore()
    expected = 0
    for cond, device in peers:
        if cond is None:
            pl.semaphore_signal(barrier, inc=1, device_id=device, device_id_type=MESH)
            expected = expected + 1
        else:
            @pl.when(cond)
            def _():
                pl.semaphore_signal(barrier, inc=1, device_id=device, device_id_type=MESH)
            expected = expected + jnp.where(cond, 1, 0)
    pl.semaphore_wait(barrier, expected)

    def send(src, dst, tx, rx, device):
        return pltpu.make_async_remote_copy(
            src_ref=src, dst_ref=dst, send_sem=tx, recv_sem=rx, device_id=device, device_id_type=MESH
        )

    def chunk(kind, from_slot, to_slot, h, route, device):
        return send(
            buf.at[kind, from_slot, h], buf.at[kind, to_slot, h],
            tx_sem.at[kind, route, h], rx_sem.at[kind, to_slot, h], device,
        )

    def to_mate(kind, h):
        return chunk(kind, OWN, MATE, h, 0, dev(mate_b, s))

    def to_core(kind, h):
        return chunk(kind, OWN, on_slot, h, 1, dev(b, on_s))

    def to_side(kind, h):
        return chunk(kind, OWN, off_slot, h, 2, dev(b, off_s))

    def mate_to_band(kind, h):
        return chunk(kind, MATE, FAR, h, 3, dev(relay_b, s))

    def mate_to_side(kind, h):
        return chunk(kind, MATE, off_slot, h, 4, dev(mate_b, off_s))

    def arrival(kind, slot, h):
        return chunk(kind, slot, slot, h, 0, dev(mate_b, s))

    def pick_to_far(kind, h):
        return send(
            pick.at[kind, h], buf.at[kind, FAR, h], picktx_sem.at[kind, h], rx_sem.at[kind, FAR, h], dev(b, opp)
        )

    def stat(to_slot, h, route, device):
        return send(st.at[OWN, h], st.at[to_slot, h], sttx_sem.at[route, h], strx_sem.at[to_slot, h], device)

    def stat_sends(h):
        return (
            (None, stat(EAST, h, 0, dev(b, west_s))),
            (None, stat(WEST, h, 1, dev(b, east_s))),
            (None, stat(MATE, h, 2, dev(mate_b, s))),
            (has_far, stat(FAR, h, 3, dev(far_b, s))),
            (polar, stat(FAR, h, 3, dev(b, opp))),
            (polar, stat(6, h, 4, dev(b, opp_w))),
            (polar, stat(5, h, 5, dev(b, opp_e))),
        )

    def guarded(cond, action):
        if cond is None:
            action()
        else:
            pl.when(cond)(action)

    def within(h):
        return (h >= 0) & (h < heads)

    def send_own(kind, h):
        if kind == 0:
            for k in range(2):
                for which in range(2):
                    load(k, which, h).wait()
        to_mate(kind, h).start()
        to_core(kind, h).start()

    def own_sends(t):
        for kind, h in ((0, t + AHEAD), (1, t + AHEAD - LAG)):
            pl.when(within(h))(functools.partial(send_own, kind, h))

    def relay(kind, h):
        pl.when(heavy)(lambda: to_side(kind, h).start())
        arrival(kind, MATE, h).wait_recv()
        pl.when(heavy)(lambda: mate_to_side(kind, h).start())
        pl.when(has_relay)(lambda: mate_to_band(kind, h).start())

    def collect(kind, h):
        arrival(kind, WEST, h).wait_recv()
        arrival(kind, EAST, h).wait_recv()

        @pl.when(polar)
        def _():
            for which in range(2):
                total = buf[kind, OWN, h, which].astype(jnp.float32) * flag[3 * kind, 0:1, :]
                total += buf[kind, WEST, h, which].astype(jnp.float32) * flag[3 * kind + 1, 0:1, :]
                total += buf[kind, EAST, h, which].astype(jnp.float32) * flag[3 * kind + 2, 0:1, :]
                pick[kind, h, which] = total.astype(jnp.bfloat16)
            pick_to_far(kind, h).start()

    def attend(h):
        arrival(0, FAR, h).wait_recv()
        query = buf[1, OWN, h, 0]
        cotan = buf[1, OWN, h, 1]
        keys = buf[0, :, h, 0].reshape(5 * DH, DH)
        values = buf[0, :, h, 1].reshape(5 * DH, DH)
        scores = nt(query, keys) * scale + bias[0, 0:1, :]
        highest = jnp.max(scores, axis=1, keepdims=True)
        grown = jnp.exp(scores - highest)
        total = jnp.sum(grown, axis=1, keepdims=True)
        probability = grown * (1.0 / total)
        attended = nn(probability.astype(jnp.bfloat16), values).astype(jnp.bfloat16)
        delta = jnp.sum(cotan.astype(jnp.float32) * attended.astype(jnp.float32), axis=1, keepdims=True)
        lse = highest + jnp.log(total)
        lane = lax.broadcasted_iota(jnp.int32, (DH, DH), 1)
        both = jnp.where(lane < 4, jnp.broadcast_to(lse, (DH, DH)), jnp.broadcast_to(delta, (DH, DH)))
        st[OWN, h] = jnp.transpose(both)[0:8, :]
        for cond, copy in stat_sends(h):
            guarded(cond, copy.start)
        out_o[:, columns(h)] = attended
        dprob = nt(cotan, values)
        dscore = (probability * (dprob - delta)).astype(jnp.bfloat16)
        out_dq[:, columns(h)] = (nn(dscore, keys) * scale).astype(jnp.bfloat16)

    def terms(h, first, count, rows):
        def row(i):
            return jnp.concatenate([r[i : i + 1, :] for r in rows], axis=1)

        shift = bias[1, 0:1, first * DH : (first + count) * DH] - row(0)
        queries = buf[1, first : first + count, h, 0].reshape(count * DH, DH)
        cotans = buf[1, first : first + count, h, 1].reshape(count * DH, DH)
        probability = jnp.exp(nt(buf[0, OWN, h, 0], queries) * scale + shift)
        dscore = (probability * (nt(buf[0, OWN, h, 1], cotans) - row(4))).astype(jnp.bfloat16)
        return nn(dscore, queries), nn(probability.astype(jnp.bfloat16), cotans)

    def spread_near(h):
        for slot in (WEST, EAST, MATE):
            stat(slot, h, 0, dev(mate_b, s)).wait_recv()
        key_sum, value_sum = terms(h, OWN, 4, [st[slot, h] for slot in (OWN, WEST, EAST, MATE)])
        near[h % 7, 0] = key_sum
        near[h % 7, 1] = value_sum

    def spread_far(h):
        arrival(1, FAR, h).wait_recv()
        stat(FAR, h, 0, dev(mate_b, s)).wait_recv()
        pl.when(~polar)(lambda: far_st.__setitem__(Ellipsis, st[FAR, h]))

        @pl.when(polar)
        def _():
            for slot in (5, 6):
                stat(slot, h, 0, dev(mate_b, s)).wait_recv()
            chosen = jnp.where(flag[6, :, :] > 0.5, st[5, h], st[FAR, h])
            far_st[...] = jnp.where(flag[7, :, :] > 0.5, st[6, h], chosen)

        key_sum, value_sum = terms(h, FAR, 1, [far_st[...]])
        out_dk[:, columns(h)] = ((near[h % 7, 0] + key_sum) * scale).astype(jnp.bfloat16)
        out_dv[:, columns(h)] = (near[h % 7, 1] + value_sum).astype(jnp.bfloat16)

    def spread(t):
        pl.when(within(t - LAG))(lambda: spread_near(t - LAG))
        late = jnp.where(polar, FAR_LATE, 0)
        pl.when(within(t - LAG - late))(lambda: spread_far(t - LAG - late))

    def relays(t):
        for kind, h in ((0, t + SIDE), (1, t + SIDE - LAG)):
            pl.when(within(h))(functools.partial(relay, kind, h))

    @pl.loop(0, AHEAD)
    def _(t):
        own_sends(t - AHEAD)

    @pl.loop(0, SIDE)
    def _(t):
        relays(t - SIDE)

    for copy in tables:
        copy.wait()

    ids = [b * lon + s, b * lon + west_s, b * lon + east_s, mate_b * lon + s, far_b * lon + s]
    table = nb[...].astype(jnp.float32)
    lanes = lax.broadcasted_iota(jnp.int32, table.shape, 1)

    def lists(tile, other):
        row = jnp.sum(jnp.where(lanes == tile, table, 0.0), axis=1, keepdims=True)
        hit = jnp.where(row == other.astype(jnp.float32), 1.0, 0.0)
        return jnp.max(hit, axis=0, keepdims=True)

    def as_bias(parts):
        polar_one = jnp.where(polar, 1.0, 0.0)
        parts[FAR] = jnp.maximum(parts[FAR], polar_one)
        whole = jnp.concatenate([jnp.broadcast_to(p, (8, DH)) for p in parts], axis=1)
        return jnp.where(whole > 0.5, 0.0, NEG)

    bias[0] = as_bias([lists(ids[0], other) for other in ids])
    bias[1] = as_bias([lists(other, ids[0]) for other in ids])

    @pl.when(polar)
    def _():
        across = pt[...].astype(jnp.float32)
        strip_of = lax.broadcasted_iota(jnp.int32, across.shape, 1)
        row_of = lax.broadcasted_iota(jnp.int32, across.shape, 0)
        mine = jnp.where(b == 0, 0, 1)

        def partner_is(strip, other):
            here = jnp.where((row_of == mine) & (strip_of == strip), across, 0.0)
            value = jnp.sum(jnp.sum(here, axis=1, keepdims=True), axis=0, keepdims=True)
            return jnp.broadcast_to(jnp.where(value == other.astype(jnp.float32), 1.0, 0.0), (8, DH))

        pairs = ((partner_is(opp, west_s), partner_is(opp, east_s)), (partner_is(west_s, opp), partner_is(east_s, opp)))
        for kind, (west, east) in enumerate(pairs):
            flag[3 * kind] = 1.0 - west - east
            flag[3 * kind + 1] = west
            flag[3 * kind + 2] = east
        flag[6] = partner_is(opp_w, s)
        flag[7] = partner_is(opp_e, s)

    late = jnp.where(polar, LATE, 0)

    @pl.loop(0, heads + LAG + FAR_LATE)
    def _(t):
        for kind, lag in ((0, 0), (1, LAG)):
            pl.when(within(t + AHEAD - lag))(lambda: send_own(kind, t + AHEAD - lag))
            pl.when(within(t + SIDE - lag))(lambda: relay(kind, t + SIDE - lag))
            pl.when(within(t - lag))(lambda: collect(kind, t - lag))
            if kind == 0:
                pl.when(within(t - late))(lambda: attend(t - late))
            else:
                spread(t)

    @pl.loop(0, heads)
    def _(h):
        for kind in range(2):
            to_mate(kind, h).wait_send()
            to_core(kind, h).wait_send()

            @pl.when(heavy)
            def _():
                to_side(kind, h).wait_send()
                mate_to_side(kind, h).wait_send()

            pl.when(has_relay)(lambda: mate_to_band(kind, h).wait_send())

            pl.when(polar)(lambda: pick_to_far(kind, h).wait_send())

        for cond, copy in stat_sends(h):
            guarded(cond, copy.wait_send)


def store(*refs):
    copies = [pltpu.make_async_copy(refs[i], refs[4 + i], refs[8].at[i]) for i in range(4)]
    for copy in copies:
        copy.start()
    for copy in copies:
        copy.wait()


def body(queries, keys, values, out_grad, neighbours, partner):
    lon = lax.axis_size("lon")
    lat = lax.axis_size("lat")
    shape = queries.shape
    tokens = shape[0] * shape[1]
    width = shape[2]
    heads = width // DH
    flat = [a.reshape(tokens, width) for a in (queries, keys, values, out_grad)]
    bf16 = jnp.bfloat16
    f32 = jnp.float32
    dma = pltpu.SemaphoreType.DMA
    tile = (DH, DH)
    results = pl.pallas_call(
        functools.partial(kernel, heads, lon, lat),
        out_shape=[jax.ShapeDtypeStruct((tokens, width), bf16)] * 4,
        in_specs=[pl.BlockSpec(memory_space=pltpu.HBM)] * 6,
        out_specs=[pl.BlockSpec(memory_space=pltpu.VMEM)] * 4,
        scratch_shapes=[
            pltpu.VMEM((2, 5, heads, 2) + tile, bf16),
            pltpu.VMEM((7, heads, 8, DH), f32),
            pltpu.VMEM((8, DH), f32),
            pltpu.VMEM((7, 2) + tile, f32),
            pltpu.VMEM((2, heads, 2) + tile, bf16),
            pltpu.VMEM(neighbours.shape[::-1], jnp.int32),
            pltpu.VMEM(partner.shape, jnp.int32),
            pltpu.VMEM((2, 8, 5 * DH), f32),
            pltpu.VMEM((8, 8, DH), f32),
            dma((2, 2, heads)),
            dma((2,)),
            dma((2, 5, heads)),
            dma((2, 5, heads)),
            dma((7, heads)),
            dma((6, heads)),
            dma((2, heads)),
        ],
        compiler_params=pltpu.CompilerParams(
            collective_id=0, has_side_effects=True, vmem_limit_bytes=48 * 1024 * 1024
        ),
        name="tile_attention",
    )(*[pltpu.with_memory_space_constraint(a, pltpu.HBM) for a in (*flat, neighbours.T, partner)])
    finished = pl.pallas_call(
        store,
        out_shape=[jax.ShapeDtypeStruct((tokens, width), bf16)] * 4,
        in_specs=[pl.BlockSpec(memory_space=pl.ANY)] * 4,
        out_specs=[pl.BlockSpec(memory_space=pltpu.HBM)] * 4,
        scratch_shapes=[dma((4,))],
        name="store_results",
    )(*[pltpu.with_memory_space_constraint(r, pltpu.VMEM) for r in results])
    return tuple(r.reshape(shape) for r in finished)


def solution(mesh):
    tiled = P("lat", "lon", None)
    return jax.shard_map(
        body,
        mesh=mesh,
        in_specs=(tiled, tiled, tiled, tiled, P(), P()),
        out_specs=(tiled, tiled, tiled, tiled),
        check_vma=False,
    )
```

```python
import functools

import jax
import jax.numpy as jnp
from jax import lax
from jax.experimental import pallas as pl
from jax.experimental.pallas import tpu as pltpu
from jax.sharding import PartitionSpec as P

DH = 128
NEG = -1e30
AHEAD = 4
SIDE = 2
LAG = 8
LATE = 5
FAR_LATE = 7
MESH = pl.DeviceIdType.MESH

OWN, WEST, EAST, MATE, FAR = range(5)


def nt(a, b):
    return lax.dot_general(a, b, (((1,), (1,)), ((), ())), preferred_element_type=jnp.float32)


def nn(a, b):
    return lax.dot_general(a, b, (((1,), (0,)), ((), ())), preferred_element_type=jnp.float32)


def kernel(
    heads, lon, lat,
    q_hbm, k_hbm, v_hbm, g_hbm, nb_hbm, pt_hbm,
    out_o, out_dq, out_dk, out_dv,
    buf, st, far_st, near, pick, nb, pt, bias, flag,
    ld_sem, tb_sem, rx_sem, tx_sem, strx_sem, sttx_sem, picktx_sem,
):
    s = lax.axis_index("lon")
    b = lax.axis_index("lat")
    core = s % 2
    odd = b % 2
    mate_b = b + 1 - 2 * odd
    far_b = b - 1 + 2 * odd
    relay_b = b + 2 - 4 * odd
    on_s = s + 1 - 2 * core
    off_s = (s + 2 * core - 1 + lon) % lon
    west_s = (s + lon - 1) % lon
    east_s = (s + 1) % lon
    opp = (s + lon // 2) % lon
    opp_w = (opp + lon - 1) % lon
    opp_e = (opp + 1) % lon
    on_slot = 1 + core
    off_slot = 2 - core
    heavy = odd == core
    has_relay = (relay_b >= 0) & (relay_b < lat)
    has_far = (far_b >= 0) & (far_b < lat)
    polar = (b == 0) | (b == lat - 1)
    scale = DH ** -0.5

    def dev(band, strip):
        return {"lat": band, "lon": strip}

    peers = [
        (None, dev(mate_b, s)),
        (None, dev(b, on_s)),
        (None, dev(b, off_s)),
        (has_far, dev(far_b, s)),
        (b + 2 < lat, dev(b + 2, s)),
        (b >= 2, dev(b - 2, s)),
        (heavy, dev(mate_b, off_s)),
        (polar, dev(b, opp_w)),
        (polar, dev(b, opp)),
        (polar, dev(b, opp_e)),
    ]

    def columns(h):
        return pl.ds(pl.multiple_of(h * DH, DH), DH)

    sources = ((k_hbm, v_hbm), (q_hbm, g_hbm))

    def load(kind, which, h):
        return pltpu.make_async_copy(
            sources[kind][which].at[:, columns(h)], buf.at[kind, OWN, h, which], ld_sem.at[kind, which, h]
        )

    @pl.loop(0, heads)
    def _(h):
        for kind in range(2):
            for which in range(2):
                load(kind, which, h).start()

    tables = (pltpu.make_async_copy(nb_hbm, nb, tb_sem.at[0]), pltpu.make_async_copy(pt_hbm, pt, tb_sem.at[1]))
    for copy in tables:
        copy.start()

    barrier = pltpu.get_barrier_semaphore()
    expected = 0
    for cond, device in peers:
        if cond is None:
            pl.semaphore_signal(barrier, inc=1, device_id=device, device_id_type=MESH)
            expected = expected + 1
        else:
            @pl.when(cond)
            def _():
                pl.semaphore_signal(barrier, inc=1, device_id=device, device_id_type=MESH)
            expected = expected + jnp.where(cond, 1, 0)
    pl.semaphore_wait(barrier, expected)

    def send(src, dst, tx, rx, device):
        return pltpu.make_async_remote_copy(
            src_ref=src, dst_ref=dst, send_sem=tx, recv_sem=rx, device_id=device, device_id_type=MESH
        )

    def chunk(kind, from_slot, to_slot, h, route, device):
        return send(
            buf.at[kind, from_slot, h], buf.at[kind, to_slot, h],
            tx_sem.at[kind, route, h], rx_sem.at[kind, to_slot, h], device,
        )

    def to_mate(kind, h):
        return chunk(kind, OWN, MATE, h, 0, dev(mate_b, s))

    def to_core(kind, h):
        return chunk(kind, OWN, on_slot, h, 1, dev(b, on_s))

    def to_side(kind, h):
        return chunk(kind, OWN, off_slot, h, 2, dev(b, off_s))

    def mate_to_band(kind, h):
        return chunk(kind, MATE, FAR, h, 3, dev(relay_b, s))

    def mate_to_side(kind, h):
        return chunk(kind, MATE, off_slot, h, 4, dev(mate_b, off_s))

    def arrival(kind, slot, h):
        return chunk(kind, slot, slot, h, 0, dev(mate_b, s))

    def pick_to_far(kind, h):
        return send(
            pick.at[kind, h], buf.at[kind, FAR, h], picktx_sem.at[kind, h], rx_sem.at[kind, FAR, h], dev(b, opp)
        )

    def stat(to_slot, h, route, device):
        return send(st.at[OWN, h], st.at[to_slot, h], sttx_sem.at[route, h], strx_sem.at[to_slot, h], device)

    def stat_sends(h):
        return (
            (None, stat(EAST, h, 0, dev(b, west_s))),
            (None, stat(WEST, h, 1, dev(b, east_s))),
            (None, stat(MATE, h, 2, dev(mate_b, s))),
            (has_far, stat(FAR, h, 3, dev(far_b, s))),
            (polar, stat(FAR, h, 3, dev(b, opp))),
            (polar, stat(6, h, 4, dev(b, opp_w))),
            (polar, stat(5, h, 5, dev(b, opp_e))),
        )

    def guarded(cond, action):
        if cond is None:
            action()
        else:
            pl.when(cond)(action)

    def within(h):
        return (h >= 0) & (h < heads)

    def send_own(kind, h):
        if kind == 0:
            for k in range(2):
                for which in range(2):
                    load(k, which, h).wait()
        to_mate(kind, h).start()
        to_core(kind, h).start()

    def own_sends(t):
        for kind, h in ((0, t + AHEAD), (1, t + AHEAD - LAG)):
            pl.when(within(h))(functools.partial(send_own, kind, h))

    def relay(kind, h):
        pl.when(heavy)(lambda: to_side(kind, h).start())
        arrival(kind, MATE, h).wait_recv()
        pl.when(heavy)(lambda: mate_to_side(kind, h).start())
        pl.when(has_relay)(lambda: mate_to_band(kind, h).start())

    def collect(kind, h):
        arrival(kind, WEST, h).wait_recv()
        arrival(kind, EAST, h).wait_recv()

        @pl.when(polar)
        def _():
            for which in range(2):
                total = buf[kind, OWN, h, which].astype(jnp.float32) * flag[3 * kind, 0:1, :]
                total += buf[kind, WEST, h, which].astype(jnp.float32) * flag[3 * kind + 1, 0:1, :]
                total += buf[kind, EAST, h, which].astype(jnp.float32) * flag[3 * kind + 2, 0:1, :]
                pick[kind, h, which] = total.astype(jnp.bfloat16)
            pick_to_far(kind, h).start()

    def attend(h):
        arrival(0, FAR, h).wait_recv()
        query = buf[1, OWN, h, 0]
        cotan = buf[1, OWN, h, 1]
        keys = buf[0, :, h, 0].reshape(5 * DH, DH)
        values = buf[0, :, h, 1].reshape(5 * DH, DH)
        scores = nt(query, keys) * scale + bias[0, 0:1, :]
        highest = jnp.max(scores, axis=1, keepdims=True)
        grown = jnp.exp(scores - highest)
        total = jnp.sum(grown, axis=1, keepdims=True)
        probability = grown * (1.0 / total)
        attended = nn(probability.astype(jnp.bfloat16), values).astype(jnp.bfloat16)
        delta = jnp.sum(cotan.astype(jnp.float32) * attended.astype(jnp.float32), axis=1, keepdims=True)
        lse = highest + jnp.log(total)
        lane = lax.broadcasted_iota(jnp.int32, (DH, DH), 1)
        both = jnp.where(lane < 4, jnp.broadcast_to(lse, (DH, DH)), jnp.broadcast_to(delta, (DH, DH)))
        st[OWN, h] = jnp.transpose(both)[0:8, :]
        for cond, copy in stat_sends(h):
            guarded(cond, copy.start)
        out_o[:, columns(h)] = attended
        dprob = nt(cotan, values)
        dscore = (probability * (dprob - delta)).astype(jnp.bfloat16)
        out_dq[:, columns(h)] = (nn(dscore, keys) * scale).astype(jnp.bfloat16)

    def terms(h, first, count, rows):
        def row(i):
            return jnp.concatenate([r[i : i + 1, :] for r in rows], axis=1)

        shift = bias[1, 0:1, first * DH : (first + count) * DH] - row(0)
        queries = buf[1, first : first + count, h, 0].reshape(count * DH, DH)
        cotans = buf[1, first : first + count, h, 1].reshape(count * DH, DH)
        probability = jnp.exp(nt(buf[0, OWN, h, 0], queries) * scale + shift)
        dscore = (probability * (nt(buf[0, OWN, h, 1], cotans) - row(4))).astype(jnp.bfloat16)
        return nn(dscore, queries), nn(probability.astype(jnp.bfloat16), cotans)

    def spread_near(h):
        for slot in (WEST, EAST, MATE):
            stat(slot, h, 0, dev(mate_b, s)).wait_recv()
        key_sum, value_sum = terms(h, OWN, 4, [st[slot, h] for slot in (OWN, WEST, EAST, MATE)])
        near[h % 8, 0] = key_sum
        near[h % 8, 1] = value_sum

    def spread_far(h):
        arrival(1, FAR, h).wait_recv()
        stat(FAR, h, 0, dev(mate_b, s)).wait_recv()
        pl.when(~polar)(lambda: far_st.__setitem__(Ellipsis, st[FAR, h]))

        @pl.when(polar)
        def _():
            for slot in (5, 6):
                stat(slot, h, 0, dev(mate_b, s)).wait_recv()
            chosen = jnp.where(flag[6, :, :] > 0.5, st[5, h], st[FAR, h])
            far_st[...] = jnp.where(flag[7, :, :] > 0.5, st[6, h], chosen)

        key_sum, value_sum = terms(h, FAR, 1, [far_st[...]])
        out_dk[:, columns(h)] = ((near[h % 8, 0] + key_sum) * scale).astype(jnp.bfloat16)
        out_dv[:, columns(h)] = (near[h % 8, 1] + value_sum).astype(jnp.bfloat16)

    def spread(t):
        pl.when(within(t - LAG))(lambda: spread_near(t - LAG))
        late = jnp.where(polar, FAR_LATE, 0)
        pl.when(within(t - LAG - late))(lambda: spread_far(t - LAG - late))

    def relays(t):
        for kind, h in ((0, t + SIDE), (1, t + SIDE - LAG)):
            pl.when(within(h))(functools.partial(relay, kind, h))

    @pl.loop(0, AHEAD)
    def _(t):
        own_sends(t - AHEAD)

    @pl.loop(0, SIDE)
    def _(t):
        relays(t - SIDE)

    for copy in tables:
        copy.wait()

    ids = [b * lon + s, b * lon + west_s, b * lon + east_s, mate_b * lon + s, far_b * lon + s]
    table = nb[...].astype(jnp.float32)
    lanes = lax.broadcasted_iota(jnp.int32, table.shape, 1)

    def lists(tile, other):
        row = jnp.sum(jnp.where(lanes == tile, table, 0.0), axis=1, keepdims=True)
        hit = jnp.where(row == other.astype(jnp.float32), 1.0, 0.0)
        return jnp.max(hit, axis=0, keepdims=True)

    def as_bias(parts):
        polar_one = jnp.where(polar, 1.0, 0.0)
        parts[FAR] = jnp.maximum(parts[FAR], polar_one)
        whole = jnp.concatenate([jnp.broadcast_to(p, (8, DH)) for p in parts], axis=1)
        return jnp.where(whole > 0.5, 0.0, NEG)

    bias[0] = as_bias([lists(ids[0], other) for other in ids])
    bias[1] = as_bias([lists(other, ids[0]) for other in ids])

    @pl.when(polar)
    def _():
        across = pt[...].astype(jnp.float32)
        strip_of = lax.broadcasted_iota(jnp.int32, across.shape, 1)
        row_of = lax.broadcasted_iota(jnp.int32, across.shape, 0)
        mine = jnp.where(b == 0, 0, 1)

        def partner_is(strip, other):
            here = jnp.where((row_of == mine) & (strip_of == strip), across, 0.0)
            value = jnp.sum(jnp.sum(here, axis=1, keepdims=True), axis=0, keepdims=True)
            return jnp.broadcast_to(jnp.where(value == other.astype(jnp.float32), 1.0, 0.0), (8, DH))

        pairs = ((partner_is(opp, west_s), partner_is(opp, east_s)), (partner_is(west_s, opp), partner_is(east_s, opp)))
        for kind, (west, east) in enumerate(pairs):
            flag[3 * kind] = 1.0 - west - east
            flag[3 * kind + 1] = west
            flag[3 * kind + 2] = east
        flag[6] = partner_is(opp_w, s)
        flag[7] = partner_is(opp_e, s)

    late = jnp.where(polar, LATE, 0)

    @pl.loop(0, heads + LAG + FAR_LATE)
    def _(t):
        for kind, lag in ((0, 0), (1, LAG)):
            pl.when(within(t + AHEAD - lag))(lambda: send_own(kind, t + AHEAD - lag))
            pl.when(within(t + SIDE - lag))(lambda: relay(kind, t + SIDE - lag))
            pl.when(within(t - lag))(lambda: collect(kind, t - lag))
            if kind == 0:
                pl.when(within(t - late))(lambda: attend(t - late))
            else:
                spread(t)

    @pl.loop(0, heads)
    def _(h):
        for kind in range(2):
            to_mate(kind, h).wait_send()
            to_core(kind, h).wait_send()

            @pl.when(heavy)
            def _():
                to_side(kind, h).wait_send()
                mate_to_side(kind, h).wait_send()

            pl.when(has_relay)(lambda: mate_to_band(kind, h).wait_send())

            pl.when(polar)(lambda: pick_to_far(kind, h).wait_send())

        for cond, copy in stat_sends(h):
            guarded(cond, copy.wait_send)


def store(*refs):
    copies = [pltpu.make_async_copy(refs[i], refs[4 + i], refs[8].at[i]) for i in range(4)]
    for copy in copies:
        copy.start()
    for copy in copies:
        copy.wait()


def body(queries, keys, values, out_grad, neighbours, partner):
    lon = lax.axis_size("lon")
    lat = lax.axis_size("lat")
    shape = queries.shape
    tokens = shape[0] * shape[1]
    width = shape[2]
    heads = width // DH
    flat = [a.reshape(tokens, width) for a in (queries, keys, values, out_grad)]
    bf16 = jnp.bfloat16
    f32 = jnp.float32
    dma = pltpu.SemaphoreType.DMA
    tile = (DH, DH)
    results = pl.pallas_call(
        functools.partial(kernel, heads, lon, lat),
        out_shape=[jax.ShapeDtypeStruct((tokens, width), bf16)] * 4,
        in_specs=[pl.BlockSpec(memory_space=pltpu.HBM)] * 6,
        out_specs=[pl.BlockSpec(memory_space=pltpu.VMEM)] * 4,
        scratch_shapes=[
            pltpu.VMEM((2, 5, heads, 2) + tile, bf16),
            pltpu.VMEM((7, heads, 8, DH), f32),
            pltpu.VMEM((8, DH), f32),
            pltpu.VMEM((8, 2) + tile, f32),
            pltpu.VMEM((2, heads, 2) + tile, bf16),
            pltpu.VMEM(neighbours.shape[::-1], jnp.int32),
            pltpu.VMEM(partner.shape, jnp.int32),
            pltpu.VMEM((2, 8, 5 * DH), f32),
            pltpu.VMEM((8, 8, DH), f32),
            dma((2, 2, heads)),
            dma((2,)),
            dma((2, 5, heads)),
            dma((2, 5, heads)),
            dma((7, heads)),
            dma((6, heads)),
            dma((2, heads)),
        ],
        compiler_params=pltpu.CompilerParams(
            collective_id=0, has_side_effects=True, vmem_limit_bytes=48 * 1024 * 1024
        ),
        name="tile_attention",
    )(*[pltpu.with_memory_space_constraint(a, pltpu.HBM) for a in (*flat, neighbours.T, partner)])
    finished = pl.pallas_call(
        store,
        out_shape=[jax.ShapeDtypeStruct((tokens, width), bf16)] * 4,
        in_specs=[pl.BlockSpec(memory_space=pl.ANY)] * 4,
        out_specs=[pl.BlockSpec(memory_space=pltpu.HBM)] * 4,
        scratch_shapes=[dma((4,))],
        name="store_results",
    )(*[pltpu.with_memory_space_constraint(r, pltpu.VMEM) for r in results])
    return tuple(r.reshape(shape) for r in finished)


def solution(mesh):
    tiled = P("lat", "lon", None)
    return jax.shard_map(
        body,
        mesh=mesh,
        in_specs=(tiled, tiled, tiled, tiled, P(), P()),
        out_specs=(tiled, tiled, tiled, tiled),
        check_vma=False,
    )
```
